256 devices in a mesh: dp: 8 (over x, y_lo), fsdp: 16 (over z, core), tensor: 2 (over y_hi).
Axes of the slice: x: 4, y: 4 (y_hi: 2, y_lo: 2; y = y_hi * 2 + y_lo), z: 8, core: 2. Of those that a mesh axis runs over, the one named last changes fastest.
Arguments:
- pooled: bfloat16 [8, 3072, 1152], P('dp', 'fsdp'), may hold values from -6 to 6
- ln_gain: float32 [1152], replicated, may hold values from 0.5 to 1.5
- w_in: bfloat16 [1152, 4304], P('fsdp', 'tensor'), may hold values from -0.1875 to 0.1875
- w_out: bfloat16 [4304, 1152], P('tensor', 'fsdp'), may hold values from -0.09375 to 0.09375
- texts: bfloat16 [8, 3072, 1152], P('dp', ('fsdp', 'tensor')), may hold values from -6 to 6
Outputs:
- grad_pooled: float32 [8, 3072, 1152], P('dp', 'fsdp')
- grad_in: float32 [1152, 4304], P('fsdp', 'tensor')
- grad_out: float32 [4304, 1152], P('tensor', 'fsdp')
The draws below stay inside these ranges and needn't reach their ends.
All inputs are finite; a program needn't handle non-finite values.
Results may differ from the reference program's by a relative error of at most 0.022.
Values may be sent and summed in bfloat16 or wider, within the bound.
A program may use at most 64 MiB of HBM per device.

```python
import jax
import jax.numpy as jnp
from jax import lax

D = 1152
FF = 4304
IMG_DEV = 192
GROUP = 3072
GROUPS = 8
N_FSDP = 16


def levels(own_key, dims, cuts, least, largest):
    def one(axis_at, blocks):
        steps = jax.random.uniform(jax.random.fold_in(jax.random.fold_in(own_key, 6), axis_at), (blocks,), jnp.float32, least / len(cuts), largest / len(cuts))
        return jnp.repeat(jnp.exp(steps), dims[axis_at] // blocks).reshape((-1,) + (1,) * (len(dims) - axis_at - 1))

    gain = one(*cuts[0])
    for cut in cuts[1:]:
        gain = gain * one(*cut)
    return gain


def noise(stream_key, shape, width, most, shards=(), kind=jnp.bfloat16):
    entries = width * jax.random.normal(stream_key, shape, jnp.float32)
    if shards:
        entries = entries * levels(stream_key, shape, shards, -0.22, 0.18)
    return jnp.clip(entries, -most, most).astype(kind)


def setup_inputs(seed: int = 0) -> dict:
    streams_of = jax.random.split(jax.random.key(seed), 6)
    return {
        "pooled": noise(streams_of[0], (GROUPS, GROUP, D), 1.0, 6.0, ((0, 8), (1, 16))),
        "ln_gain": jnp.clip(1.0 + 0.1 * jax.random.normal(streams_of[1], (D,), jnp.float32), 0.5, 1.5),
        "w_in": noise(streams_of[2], (D, FF), D ** -0.5, 0.1875, ((0, 16), (1, 2))),
        "w_out": noise(streams_of[3], (FF, D), FF ** -0.5, 0.09375, ((0, 2), (1, 16))),
        "texts": noise(streams_of[4], (GROUPS, GROUP, D), 1.0, 6.0, ((0, 8), (1, 32))),
    }


ln_eps = 1e-06
norm_eps = 1e-06
logit_scale = 10.0
logit_bias = -2.0

def gelu_tanh(values):
    return jax.nn.gelu(values, approximate=True)

def unit_rows(values):
    return values / jnp.sqrt(lax.optimization_barrier(jnp.sum(values * values, axis=-1, keepdims=True)) + norm_eps)

def rounded(values):
    return lax.optimization_barrier(values.astype(jnp.bfloat16)).astype(jnp.float32)

def one_group(pooled_group, texts_group, ln_gain, w_in, w_out):
    rows = pooled_group.astype(jnp.float32)
    row_mean = lax.optimization_barrier(jnp.mean(rows, axis=1, keepdims=True))
    centred = rows - row_mean
    inv_std = lax.rsqrt(lax.optimization_barrier(jnp.mean(centred * centred, axis=1, keepdims=True)) + ln_eps)
    normal_rows = centred * inv_std
    unit_in = (normal_rows * ln_gain).astype(jnp.bfloat16)
    pre_act = jnp.dot(unit_in, w_in, preferred_element_type=jnp.float32)
    hidden = gelu_tanh(pre_act).astype(jnp.bfloat16)
    mixed = rows + jnp.dot(hidden, w_out, preferred_element_type=jnp.float32)
    row_norm = jnp.sqrt(lax.optimization_barrier(jnp.sum(mixed * mixed, axis=1, keepdims=True)) + norm_eps)
    image_unit = mixed / row_norm
    image_b = image_unit.astype(jnp.bfloat16)
    text_b = unit_rows(texts_group.astype(jnp.float32)).astype(jnp.bfloat16)
    logits = logit_scale * jnp.dot(image_b, text_b.T, preferred_element_type=jnp.float32) + logit_bias
    match = jnp.eye(GROUP, dtype=jnp.float32)
    weights = (jax.nn.sigmoid(logits) - match).astype(jnp.bfloat16)
    grad_unit = logit_scale * jnp.dot(weights, text_b, preferred_element_type=jnp.float32)
    grad_mixed = (grad_unit - image_unit * lax.optimization_barrier(jnp.sum(image_unit * grad_unit, axis=1, keepdims=True))) / row_norm
    grad_b = grad_mixed.astype(jnp.bfloat16)
    grad_hidden = jnp.dot(grad_b, w_out.T, preferred_element_type=jnp.float32)
    _, gelu_back = jax.vjp(gelu_tanh, pre_act)
    grad_pre = gelu_back(grad_hidden)[0].astype(jnp.bfloat16)
    grad_unit_in = jnp.dot(grad_pre, w_in.T, preferred_element_type=jnp.float32)
    scaled = grad_unit_in * ln_gain
    grad_rows = inv_std * (scaled - lax.optimization_barrier(jnp.mean(scaled, axis=1, keepdims=True)) - normal_rows * lax.optimization_barrier(jnp.mean(scaled * normal_rows, axis=1, keepdims=True)))
    grad_pooled = grad_mixed + grad_rows
    return (grad_pooled, unit_in, grad_pre, hidden, grad_b)

def reference(pooled, ln_gain, w_in, w_out, texts):

    def group_step(carry, inputs):
        pooled_group, texts_group = inputs
        grad_pooled, unit_in, grad_pre, hidden, grad_b = one_group(pooled_group, texts_group, ln_gain, w_in, w_out)
        blocks = (unit_in.reshape(N_FSDP, IMG_DEV, D), grad_pre.reshape(N_FSDP, IMG_DEV, FF), hidden.reshape(N_FSDP, IMG_DEV, FF), grad_b.reshape(N_FSDP, IMG_DEV, D))

        def block_step(sums, block):
            unit_part, pre_part, hidden_part, grad_part = block
            term_in = jnp.dot(unit_part.T, pre_part, preferred_element_type=jnp.float32)
            term_out = jnp.dot(hidden_part.T, grad_part, preferred_element_type=jnp.float32)
            return ((sums[0] + rounded(term_in), sums[1] + rounded(term_out)), None)
        sums, _ = lax.scan(block_step, carry, blocks)
        return (sums, grad_pooled)
    start = (jnp.zeros((D, FF), jnp.float32), jnp.zeros((FF, D), jnp.float32))
    (grad_in, grad_out), grad_pooled = lax.scan(group_step, start, (pooled, texts))
    return (grad_pooled, grad_in, grad_out)
```

```python
import jax
import jax.numpy as jnp
from jax import lax
from jax.sharding import PartitionSpec as P

ln_eps = 1e-06
norm_eps = 1e-06
logit_scale = 10.0
logit_bias = -2.0


def passed_along(block, axis, distance):
    devices = range(lax.axis_size(axis))
    route = [((i - distance) % len(devices), i) for i in devices]
    return lax.ppermute(block, axis, route)


def swapped_sum(partial, axis):
    mine = partial.astype(jnp.bfloat16)
    other = lax.ppermute(mine, axis, [(0, 1), (1, 0)])
    return mine.astype(jnp.float32) + other.astype(jnp.float32)


def doubling_sum(parts, axis):
    size = lax.axis_size(axis)
    mine = [p.astype(jnp.bfloat16) for p in parts]
    totals = None
    bit = 1
    while bit < size:
        route = [(i, i ^ bit) for i in range(size)]
        others = [lax.ppermute(m, axis, route) for m in mine]
        totals = [m.astype(jnp.float32) + o.astype(jnp.float32) for m, o in zip(mine, others)]
        mine = [t.astype(jnp.bfloat16) for t in totals]
        bit *= 2
    return totals


def gelu_tanh(values):
    return jax.nn.gelu(values, approximate=True)


def unit_rows(values):
    return values / jnp.sqrt(jnp.sum(values * values, axis=-1, keepdims=True) + norm_eps)


def text_columns(first, number, block_rows, offset, stride):
    places = first + jnp.arange(number, dtype=jnp.int32)
    return places // block_rows * stride + offset + places % block_rows


def body(pooled, ln_gain, w_in, w_out, texts):
    rows = pooled[0].astype(jnp.float32)
    images = rows.shape[0]
    width = rows.shape[1]
    text_b = unit_rows(texts[0].astype(jnp.float32)).astype(jnp.bfloat16)
    cycle_index = lax.axis_index("fsdp")
    cycle_size = lax.axis_size("fsdp")
    offset = lax.axis_index("tensor") * text_b.shape[0]
    block_rows = text_b.shape[0]

    def source_columns(source):
        return text_columns(source * block_rows, block_rows, block_rows, offset, images)

    blocks = [text_b]
    sources = [cycle_index]
    ahead = text_b
    for step in range(1, cycle_size // 2 + 1):
        ahead = passed_along(ahead, "fsdp", 1)
        blocks.append(ahead)
        sources.append((cycle_index - step) % cycle_size)
    behind = text_b
    for step in range(1, (cycle_size - 1) // 2 + 1):
        behind = passed_along(behind, "fsdp", -1)
        blocks.append(behind)
        sources.append((cycle_index + step) % cycle_size)
    all_texts = jnp.concatenate(blocks, axis=0)
    columns = jnp.concatenate([source_columns(s) for s in sources], axis=0)

    row_mean = jnp.mean(rows, axis=1, keepdims=True)
    centred = rows - row_mean
    inv_std = lax.rsqrt(jnp.mean(centred * centred, axis=1, keepdims=True) + ln_eps)
    normal_rows = centred * inv_std
    unit_in = (normal_rows * ln_gain).astype(jnp.bfloat16)
    full_in = lax.all_gather(w_in, "fsdp", axis=0, tiled=True)
    pre_act = jnp.dot(unit_in, full_in, preferred_element_type=jnp.float32)
    hidden = gelu_tanh(pre_act).astype(jnp.bfloat16)
    full_out = lax.all_gather(w_out, "fsdp", axis=1, tiled=True)
    partial_mix = jnp.dot(hidden, full_out, preferred_element_type=jnp.float32)
    mixed = rows + swapped_sum(partial_mix, "tensor")
    row_norm = jnp.sqrt(jnp.sum(mixed * mixed, axis=1, keepdims=True) + norm_eps)
    image_unit = mixed / row_norm
    image_b = image_unit.astype(jnp.bfloat16)
    image_places = cycle_index * images + jnp.arange(images, dtype=jnp.int32)

    logits = (
        logit_scale
        * jnp.einsum("rd,cd->rc", image_b, all_texts, preferred_element_type=jnp.float32)
        + logit_bias
    )
    match = (image_places[:, None] == columns[None, :]).astype(jnp.float32)
    weights = (jax.nn.sigmoid(logits) - match).astype(jnp.bfloat16)
    running = jnp.dot(weights, all_texts, preferred_element_type=jnp.float32)
    grad_unit = swapped_sum(logit_scale * running, "tensor")
    grad_mixed = (
        grad_unit - image_unit * jnp.sum(image_unit * grad_unit, axis=1, keepdims=True)
    ) / row_norm
    grad_b = grad_mixed.astype(jnp.bfloat16)
    grad_hidden = jnp.einsum("rd,fd->rf", grad_b, full_out, preferred_element_type=jnp.float32)
    _, gelu_back = jax.vjp(gelu_tanh, pre_act)
    grad_pre = gelu_back(grad_hidden)[0].astype(jnp.bfloat16)
    partial_unit = jnp.einsum("rf,df->rd", grad_pre, full_in, preferred_element_type=jnp.float32)
    grad_unit_in = swapped_sum(partial_unit, "tensor")
    scaled = grad_unit_in * ln_gain
    grad_rows = inv_std * (
        scaled
        - jnp.mean(scaled, axis=1, keepdims=True)
        - normal_rows * jnp.mean(scaled * normal_rows, axis=1, keepdims=True)
    )
    grad_pooled = (grad_mixed + grad_rows)[None]
    grad_in_part = lax.psum_scatter(
        jnp.einsum("rd,rf->df", unit_in, grad_pre, preferred_element_type=jnp.float32).astype(
            jnp.bfloat16
        ),
        "fsdp",
        scatter_dimension=0,
        tiled=True,
    )
    out_term = jnp.einsum("rf,rd->fd", hidden, grad_b, preferred_element_type=jnp.float32)
    grad_out_part = lax.psum_scatter(
        out_term.astype(jnp.bfloat16), "fsdp", scatter_dimension=1, tiled=True
    )
    grad_in, grad_out = doubling_sum([grad_in_part, grad_out_part], "dp")
    return (grad_pooled, grad_in, grad_out)


def solution(mesh):
    placed = (
        P("dp", "fsdp", None),
        P(),
        P("fsdp", "tensor"),
        P("tensor", "fsdp"),
        P("dp", ("fsdp", "tensor"), None),
    )
    return jax.shard_map(
        body,
        mesh=mesh,
        in_specs=placed,
        out_specs=(P("dp", "fsdp", None), P("fsdp", "tensor"), P("tensor", "fsdp")),
        check_vma=False,
    )
```

```python
import jax
import jax.numpy as jnp
from jax import lax
from jax.sharding import Mesh
from jax.sharding import PartitionSpec as P

ln_eps = 1e-06
norm_eps = 1e-06
logit_scale = 10.0
logit_bias = -2.0


def passed_along(block, axis, distance):
    devices = range(lax.axis_size(axis))
    route = [((i - distance) % len(devices), i) for i in devices]
    return lax.ppermute(block, axis, route)


def core_swap(block):
    return lax.ppermute(block, "core", [(0, 1), (1, 0)])


def swapped_sum(partial, axis):
    mine = partial.astype(jnp.bfloat16)
    other = lax.ppermute(mine, axis, [(0, 1), (1, 0)])
    return mine.astype(jnp.float32) + other.astype(jnp.float32)


def doubling_sum(parts, axis):
    size = lax.axis_size(axis)
    mine = [p.astype(jnp.bfloat16) for p in parts]
    totals = None
    bit = 1
    while bit < size:
        route = [(i, i ^ bit) for i in range(size)]
        others = [lax.ppermute(m, axis, route) for m in mine]
        totals = [m.astype(jnp.float32) + o.astype(jnp.float32) for m, o in zip(mine, others)]
        mine = [t.astype(jnp.bfloat16) for t in totals]
        bit *= 2
    return totals


def parity_split(values, core, chips):
    lead = values.shape[:-1]
    blocks = values.reshape(lead + (chips, 2, values.shape[-1] // (2 * chips)))
    axis = blocks.ndim - 2
    own = lax.dynamic_index_in_dim(blocks, core, axis=axis, keepdims=False)
    other = lax.dynamic_index_in_dim(blocks, 1 - core, axis=axis, keepdims=False)
    half = lead + (values.shape[-1] // 2,)
    return own.reshape(half), other.reshape(half)


def parity_join(own, other, core, chips):
    lead = own.shape[:-1]
    shape = lead + (chips, 1, own.shape[-1] // chips)
    own = own.reshape(shape)
    other = other.reshape(shape)
    even = jnp.where(core == 0, own, other)
    odd = jnp.where(core == 0, other, own)
    return jnp.concatenate([even, odd], axis=-2).reshape(lead + (2 * own.shape[-1] * chips,))


def gelu_tanh(values):
    return jax.nn.gelu(values, approximate=True)


def unit_rows(values):
    return values / jnp.sqrt(jnp.sum(values * values, axis=-1, keepdims=True) + norm_eps)


def body(pooled, ln_gain, w_in, w_out, texts):
    rows = pooled[0].astype(jnp.float32)
    images = rows.shape[0]
    chip = lax.axis_index("z")
    chips = lax.axis_size("z")
    core = lax.axis_index("core")
    block_index = chip * 2 + core

    text_b = unit_rows(texts[0].astype(jnp.float32)).astype(jnp.bfloat16)
    block_rows = text_b.shape[0]
    offset = lax.axis_index("tensor") * block_rows
    pair = jnp.concatenate([text_b, core_swap(text_b)], axis=0)
    within = jnp.arange(block_rows, dtype=jnp.int32)

    def pair_columns(source_chip):
        first = (source_chip * 2 + core) * images + offset + within
        second = (source_chip * 2 + 1 - core) * images + offset + within
        return jnp.concatenate([first, second])

    blocks = [pair]
    sources = [chip]
    ahead = pair
    for step in range(1, chips // 2 + 1):
        ahead = passed_along(ahead, "z", 1)
        blocks.append(ahead)
        sources.append((chip - step) % chips)
    behind = pair
    for step in range(1, (chips - 1) // 2 + 1):
        behind = passed_along(behind, "z", -1)
        blocks.append(behind)
        sources.append((chip + step) % chips)
    all_texts = jnp.concatenate(blocks, axis=0)
    columns = jnp.concatenate([pair_columns(s) for s in sources], axis=0)

    own_in = lax.all_gather(w_in, "z", axis=0, tiled=True)
    other_in = core_swap(own_in)
    own_out = lax.all_gather(w_out, "z", axis=1, tiled=True)
    other_out = core_swap(own_out)

    row_mean = jnp.mean(rows, axis=1, keepdims=True)
    centred = rows - row_mean
    inv_std = lax.rsqrt(jnp.mean(centred * centred, axis=1, keepdims=True) + ln_eps)
    normal_rows = centred * inv_std
    unit_in = (normal_rows * ln_gain).astype(jnp.bfloat16)
    unit_own, unit_other = parity_split(unit_in, core, chips)
    pre_act = jnp.dot(unit_own, own_in, preferred_element_type=jnp.float32) + jnp.dot(
        unit_other, other_in, preferred_element_type=jnp.float32
    )
    hidden = gelu_tanh(pre_act).astype(jnp.bfloat16)
    mix_parts = jnp.concatenate(
        [
            jnp.dot(hidden, own_out, preferred_element_type=jnp.float32),
            jnp.dot(hidden, other_out, preferred_element_type=jnp.float32),
        ],
        axis=1,
    )
    mix_sum = swapped_sum(mix_parts, "tensor")
    half = mix_sum.shape[1] // 2
    mixed = rows + parity_join(mix_sum[:, :half], mix_sum[:, half:], core, chips)
    row_norm = jnp.sqrt(jnp.sum(mixed * mixed, axis=1, keepdims=True) + norm_eps)
    image_unit = mixed / row_norm
    image_b = image_unit.astype(jnp.bfloat16)
    image_places = block_index * images + jnp.arange(images, dtype=jnp.int32)

    logits = (
        logit_scale
        * jnp.einsum("rd,cd->rc", image_b, all_texts, preferred_element_type=jnp.float32)
        + logit_bias
    )
    match = (image_places[:, None] == columns[None, :]).astype(jnp.float32)
    weights = (jax.nn.sigmoid(logits) - match).astype(jnp.bfloat16)
    running = jnp.dot(weights, all_texts, preferred_element_type=jnp.float32)
    grad_unit = swapped_sum(logit_scale * running, "tensor")
    grad_mixed = (
        grad_unit - image_unit * jnp.sum(image_unit * grad_unit, axis=1, keepdims=True)
    ) / row_norm
    grad_b = grad_mixed.astype(jnp.bfloat16)
    grad_own, grad_other = parity_split(grad_b, core, chips)
    grad_hidden = jnp.einsum(
        "rd,fd->rf", grad_own, own_out, preferred_element_type=jnp.float32
    ) + jnp.einsum("rd,fd->rf", grad_other, other_out, preferred_element_type=jnp.float32)
    _, gelu_back = jax.vjp(gelu_tanh, pre_act)
    grad_pre = gelu_back(grad_hidden)[0].astype(jnp.bfloat16)
    unit_parts = jnp.concatenate(
        [
            jnp.einsum("rf,df->rd", grad_pre, own_in, preferred_element_type=jnp.float32),
            jnp.einsum("rf,df->rd", grad_pre, other_in, preferred_element_type=jnp.float32),
        ],
        axis=1,
    )
    unit_sum = swapped_sum(unit_parts, "tensor")
    grad_unit_in = parity_join(unit_sum[:, :half], unit_sum[:, half:], core, chips)
    scaled = grad_unit_in * ln_gain
    grad_rows = inv_std * (
        scaled
        - jnp.mean(scaled, axis=1, keepdims=True)
        - normal_rows * jnp.mean(scaled * normal_rows, axis=1, keepdims=True)
    )
    grad_pooled = (grad_mixed + grad_rows)[None]

    out_own = jnp.einsum("rf,rd->fd", hidden, grad_own, preferred_element_type=jnp.float32)
    out_other = jnp.einsum("rf,rd->fd", hidden, grad_other, preferred_element_type=jnp.float32)
    out_chip = out_own.astype(jnp.bfloat16).astype(jnp.float32) + core_swap(
        out_other.astype(jnp.bfloat16)
    ).astype(jnp.float32)
    grad_out_part = lax.psum_scatter(
        out_chip.astype(jnp.bfloat16), "z", scatter_dimension=1, tiled=True
    )
    in_own = jnp.einsum("rd,rf->df", unit_own, grad_pre, preferred_element_type=jnp.float32)
    in_other = jnp.einsum("rd,rf->df", unit_other, grad_pre, preferred_element_type=jnp.float32)
    in_chip = in_own.astype(jnp.bfloat16).astype(jnp.float32) + core_swap(
        in_other.astype(jnp.bfloat16)
    ).astype(jnp.float32)
    grad_in_part = lax.psum_scatter(
        in_chip.astype(jnp.bfloat16), "z", scatter_dimension=0, tiled=True
    )
    grad_in, grad_out = doubling_sum([grad_in_part, grad_out_part], "dp")
    return (grad_pooled, grad_in, grad_out)


def solution(mesh):
    fsdp = mesh.shape["fsdp"]
    chip_mesh = Mesh(
        mesh.devices.reshape(mesh.shape["dp"], fsdp // 2, 2, mesh.shape["tensor"]),
        ("dp", "z", "core", "tensor"),
    )
    placed = (
        P("dp", ("z", "core"), None),
        P(),
        P(("z", "core"), "tensor"),
        P("tensor", ("z", "core")),
        P("dp", ("z", "core", "tensor"), None),
    )
    return jax.shard_map(
        body,
        mesh=chip_mesh,
        in_specs=placed,
        out_specs=(
            P("dp", ("z", "core"), None),
            P(("z", "core"), "tensor"),
            P("tensor", ("z", "core")),
        ),
        check_vma=False,
    )
```

```python
import jax
import jax.numpy as jnp
from jax import lax
from jax.sharding import Mesh
from jax.sharding import PartitionSpec as P

ln_eps = 1e-06
norm_eps = 1e-06
logit_scale = 10.0
logit_bias = -2.0


def passed_along(block, axis, distance):
    devices = range(lax.axis_size(axis))
    route = [((i - distance) % len(devices), i) for i in devices]
    return lax.ppermute(block, axis, route)


def core_swap(block):
    return lax.ppermute(block, "core", [(0, 1), (1, 0)])


def swapped_sum(partial, axis):
    mine = partial.astype(jnp.bfloat16)
    other = lax.ppermute(mine, axis, [(0, 1), (1, 0)])
    return mine.astype(jnp.float32) + other.astype(jnp.float32)


def doubling_sum(parts, axis):
    size = lax.axis_size(axis)
    mine = [p.astype(jnp.bfloat16) for p in parts]
    totals = None
    bit = 1
    while bit < size:
        route = [(i, i ^ bit) for i in range(size)]
        others = [lax.ppermute(m, axis, route) for m in mine]
        totals = [m.astype(jnp.float32) + o.astype(jnp.float32) for m, o in zip(mine, others)]
        mine = [t.astype(jnp.bfloat16) for t in totals]
        bit *= 2
    return totals


def parity_split(values, core, chips):
    lead = values.shape[:-1]
    blocks = values.reshape(lead + (chips, 2, values.shape[-1] // (2 * chips)))
    axis = blocks.ndim - 2
    own = lax.dynamic_index_in_dim(blocks, core, axis=axis, keepdims=False)
    other = lax.dynamic_index_in_dim(blocks, 1 - core, axis=axis, keepdims=False)
    half = lead + (values.shape[-1] // 2,)
    return own.reshape(half), other.reshape(half)


def parity_join(own, other, core, chips):
    lead = own.shape[:-1]
    shape = lead + (chips, 1, own.shape[-1] // chips)
    own = own.reshape(shape)
    other = other.reshape(shape)
    even = jnp.where(core == 0, own, other)
    odd = jnp.where(core == 0, other, own)
    return jnp.concatenate([even, odd], axis=-2).reshape(lead + (2 * own.shape[-1] * chips,))


def gelu_tanh(values):
    return jax.nn.gelu(values, approximate=True)


def unit_rows(values):
    return values / jnp.sqrt(jnp.sum(values * values, axis=-1, keepdims=True) + norm_eps)


def body(pooled, ln_gain, w_in, w_out, texts):
    rows = pooled[0].astype(jnp.float32)
    images = rows.shape[0]
    chip = lax.axis_index("z")
    chips = lax.axis_size("z")
    core = lax.axis_index("core")
    block_index = chip * 2 + core

    text_b = unit_rows(texts[0].astype(jnp.float32)).astype(jnp.bfloat16)
    block_rows = text_b.shape[0]
    offset = lax.axis_index("tensor") * block_rows
    pair = jnp.concatenate([text_b, core_swap(text_b)], axis=0)
    within = jnp.arange(block_rows, dtype=jnp.int32)

    def pair_columns(source_chip):
        first = (source_chip * 2 + core) * images + offset + within
        second = (source_chip * 2 + 1 - core) * images + offset + within
        return jnp.concatenate([first, second])

    blocks = [pair]
    sources = [chip]
    ahead = pair
    for step in range(1, chips // 2 + 1):
        ahead = passed_along(ahead, "z", 1)
        blocks.append(ahead)
        sources.append((chip - step) % chips)
    behind = pair
    for step in range(1, (chips - 1) // 2 + 1):
        behind = passed_along(behind, "z", -1)
        blocks.append(behind)
        sources.append((chip + step) % chips)
    all_texts = jnp.concatenate(blocks, axis=0)
    columns = jnp.concatenate([pair_columns(s) for s in sources], axis=0)

    stacked = jnp.stack([w_in, w_out.T])
    own_w = lax.all_gather(stacked, "z", axis=1, tiled=True)
    other_w = core_swap(own_w)
    own_in, own_out = own_w[0], own_w[1]
    other_in, other_out = other_w[0], other_w[1]

    row_mean = jnp.mean(rows, axis=1, keepdims=True)
    centred = rows - row_mean
    inv_std = lax.rsqrt(jnp.mean(centred * centred, axis=1, keepdims=True) + ln_eps)
    normal_rows = centred * inv_std
    unit_in = (normal_rows * ln_gain).astype(jnp.bfloat16)
    unit_own, unit_other = parity_split(unit_in, core, chips)
    pre_act = jnp.dot(unit_own, own_in, preferred_element_type=jnp.float32) + jnp.dot(
        unit_other, other_in, preferred_element_type=jnp.float32
    )
    hidden = gelu_tanh(pre_act).astype(jnp.bfloat16)
    mix_parts = jnp.concatenate(
        [
            jnp.einsum("rf,df->rd", hidden, own_out, preferred_element_type=jnp.float32),
            jnp.einsum("rf,df->rd", hidden, other_out, preferred_element_type=jnp.float32),
        ],
        axis=1,
    )
    mix_sum = swapped_sum(mix_parts, "tensor")
    half = mix_sum.shape[1] // 2
    mixed = rows + parity_join(mix_sum[:, :half], mix_sum[:, half:], core, chips)
    row_norm = jnp.sqrt(jnp.sum(mixed * mixed, axis=1, keepdims=True) + norm_eps)
    image_unit = mixed / row_norm
    image_b = image_unit.astype(jnp.bfloat16)
    image_places = block_index * images + jnp.arange(images, dtype=jnp.int32)

    logits = (
        logit_scale
        * jnp.einsum("rd,cd->rc", image_b, all_texts, preferred_element_type=jnp.float32)
        + logit_bias
    )
    match = (image_places[:, None] == columns[None, :]).astype(jnp.float32)
    weights = (jax.nn.sigmoid(logits) - match).astype(jnp.bfloat16)
    running = jnp.dot(weights, all_texts, preferred_element_type=jnp.float32)
    grad_unit = swapped_sum(logit_scale * running, "tensor")
    grad_mixed = (
        grad_unit - image_unit * jnp.sum(image_unit * grad_unit, axis=1, keepdims=True)
    ) / row_norm
    grad_b = grad_mixed.astype(jnp.bfloat16)
    grad_own, grad_other = parity_split(grad_b, core, chips)
    grad_hidden = jnp.einsum(
        "rd,df->rf", grad_own, own_out, preferred_element_type=jnp.float32
    ) + jnp.einsum("rd,df->rf", grad_other, other_out, preferred_element_type=jnp.float32)
    _, gelu_back = jax.vjp(gelu_tanh, pre_act)
    grad_pre = gelu_back(grad_hidden)[0].astype(jnp.bfloat16)
    unit_parts = jnp.concatenate(
        [
            jnp.einsum("rf,df->rd", grad_pre, own_in, preferred_element_type=jnp.float32),
            jnp.einsum("rf,df->rd", grad_pre, other_in, preferred_element_type=jnp.float32),
        ],
        axis=1,
    )
    unit_sum = swapped_sum(unit_parts, "tensor")
    grad_unit_in = parity_join(unit_sum[:, :half], unit_sum[:, half:], core, chips)
    scaled = grad_unit_in * ln_gain
    grad_rows = inv_std * (
        scaled
        - jnp.mean(scaled, axis=1, keepdims=True)
        - normal_rows * jnp.mean(scaled * normal_rows, axis=1, keepdims=True)
    )
    grad_pooled = (grad_mixed + grad_rows)[None]

    terms_own = jnp.stack(
        [
            jnp.einsum("rd,rf->df", unit_own, grad_pre, preferred_element_type=jnp.float32),
            jnp.einsum("rd,rf->df", grad_own, hidden, preferred_element_type=jnp.float32),
        ]
    )
    terms_other = jnp.stack(
        [
            jnp.einsum("rd,rf->df", unit_other, grad_pre, preferred_element_type=jnp.float32),
            jnp.einsum("rd,rf->df", grad_other, hidden, preferred_element_type=jnp.float32),
        ]
    )
    terms_chip = terms_own.astype(jnp.bfloat16).astype(jnp.float32) + core_swap(
        terms_other.astype(jnp.bfloat16)
    ).astype(jnp.float32)
    terms_part = lax.psum_scatter(
        terms_chip.astype(jnp.bfloat16), "z", scatter_dimension=1, tiled=True
    )
    (total,) = doubling_sum([terms_part], "dp")
    grad_in = total[0]
    grad_out = total[1].T
    return (grad_pooled, grad_in, grad_out)


def solution(mesh):
    fsdp = mesh.shape["fsdp"]
    chip_mesh = Mesh(
        mesh.devices.reshape(mesh.shape["dp"], fsdp // 2, 2, mesh.shape["tensor"]),
        ("dp", "z", "core", "tensor"),
    )
    placed = (
        P("dp", ("z", "core"), None),
        P(),
        P(("z", "core"), "tensor"),
        P("tensor", ("z", "core")),
        P("dp", ("z", "core", "tensor"), None),
    )
    return jax.shard_map(
        body,
        mesh=chip_mesh,
        in_specs=placed,
        out_specs=(
            P("dp", ("z", "core"), None),
            P(("z", "core"), "tensor"),
            P("tensor", ("z", "core")),
        ),
        check_vma=False,
    )
```

```python
import jax
import jax.numpy as jnp
from jax import lax
from jax.sharding import Mesh
from jax.sharding import PartitionSpec as P


ln_eps = 1e-06
norm_eps = 1e-06
logit_scale = 10.0
logit_bias = -2.0


def passed_along(block, axis, distance):
    devices = range(lax.axis_size(axis))
    route = [((i - distance) % len(devices), i) for i in devices]
    return lax.ppermute(block, axis, route)


def core_swap(block):
    return lax.ppermute(block, "core", [(0, 1), (1, 0)])


def swapped_sum(partial, axis):
    mine = partial.astype(jnp.bfloat16)
    other = lax.ppermute(mine, axis, [(0, 1), (1, 0)])
    return mine.astype(jnp.float32) + other.astype(jnp.float32)


def doubling_sum(parts, axis):
    size = lax.axis_size(axis)
    mine = [p.astype(jnp.bfloat16) for p in parts]
    totals = None
    bit = 1
    while bit < size:
        route = [(i, i ^ bit) for i in range(size)]
        others = [lax.ppermute(m, axis, route) for m in mine]
        totals = [m.astype(jnp.float32) + o.astype(jnp.float32) for m, o in zip(mine, others)]
        mine = [t.astype(jnp.bfloat16) for t in totals]
        bit *= 2
    return totals


def parity_split(values, core, chips):
    lead = values.shape[:-1]
    blocks = values.reshape(lead + (chips, 2, values.shape[-1] // (2 * chips)))
    axis = blocks.ndim - 2
    own = lax.dynamic_index_in_dim(blocks, core, axis=axis, keepdims=False)
    other = lax.dynamic_index_in_dim(blocks, 1 - core, axis=axis, keepdims=False)
    half = lead + (values.shape[-1] // 2,)
    return own.reshape(half), other.reshape(half)


def parity_join(own, other, core, chips):
    lead = own.shape[:-1]
    shape = lead + (chips, 1, own.shape[-1] // chips)
    own = own.reshape(shape)
    other = other.reshape(shape)
    even = jnp.where(core == 0, own, other)
    odd = jnp.where(core == 0, other, own)
    return jnp.concatenate([even, odd], axis=-2).reshape(lead + (2 * own.shape[-1] * chips,))


def gelu_tanh(values):
    return jax.nn.gelu(values, approximate=True)


def unit_rows(values):
    return values / jnp.sqrt(jnp.sum(values * values, axis=-1, keepdims=True) + norm_eps)


def layer(pooled, ln_gain, w_in, w_out, texts):
    rows = pooled[0].astype(jnp.float32)
    images = rows.shape[0]
    chip = lax.axis_index("z")
    chips = lax.axis_size("z")
    core = lax.axis_index("core")
    block_index = chip * 2 + core

    text_b = unit_rows(texts[0].astype(jnp.float32)).astype(jnp.bfloat16)
    block_rows = text_b.shape[0]
    offset = lax.axis_index("tensor") * block_rows
    pair = jnp.concatenate([text_b, core_swap(text_b)], axis=0)
    within = jnp.arange(block_rows, dtype=jnp.int32)

    def pair_columns(source_chip):
        first = (source_chip * 2 + core) * images + offset + within
        second = (source_chip * 2 + 1 - core) * images + offset + within
        return jnp.concatenate([first, second])

    blocks = [pair]
    sources = [chip]
    ahead = pair
    for step in range(1, chips // 2 + 1):
        ahead = passed_along(ahead, "z", 1)
        blocks.append(ahead)
        sources.append((chip - step) % chips)
    behind = pair
    for step in range(1, (chips - 1) // 2 + 1):
        behind = passed_along(behind, "z", -1)
        blocks.append(behind)
        sources.append((chip + step) % chips)
    all_texts = jnp.concatenate(blocks, axis=0)
    columns = jnp.concatenate([pair_columns(s) for s in sources], axis=0)

    stacked = jnp.stack([w_in, w_out.T])
    own_w = lax.all_gather(stacked, "z", axis=1, tiled=True)
    other_w = core_swap(own_w)
    own_in, own_out = own_w[0], own_w[1]
    other_in, other_out = other_w[0], other_w[1]

    row_mean = jnp.mean(rows, axis=1, keepdims=True)
    centred = rows - row_mean
    inv_std = lax.rsqrt(jnp.mean(centred * centred, axis=1, keepdims=True) + ln_eps)
    normal_rows = centred * inv_std
    unit_in = (normal_rows * ln_gain).astype(jnp.bfloat16)
    unit_own, unit_other = parity_split(unit_in, core, chips)
    pre_act = jnp.dot(unit_own, own_in, preferred_element_type=jnp.float32) + jnp.dot(
        unit_other, other_in, preferred_element_type=jnp.float32
    )
    hidden = gelu_tanh(pre_act).astype(jnp.bfloat16)
    mix_parts = jnp.concatenate(
        [
            jnp.einsum("rf,df->rd", hidden, own_out, preferred_element_type=jnp.float32),
            jnp.einsum("rf,df->rd", hidden, other_out, preferred_element_type=jnp.float32),
        ],
        axis=1,
    )
    mix_sum = swapped_sum(mix_parts, "tensor")
    half = mix_sum.shape[1] // 2
    mixed = rows + parity_join(mix_sum[:, :half], mix_sum[:, half:], core, chips)
    row_norm = jnp.sqrt(jnp.sum(mixed * mixed, axis=1, keepdims=True) + norm_eps)
    image_unit = mixed / row_norm
    image_b = image_unit.astype(jnp.bfloat16)
    image_places = block_index * images + jnp.arange(images, dtype=jnp.int32)

    logits = (
        logit_scale
        * jnp.einsum("rd,cd->rc", image_b, all_texts, preferred_element_type=jnp.float32)
        + logit_bias
    )
    match = (image_places[:, None] == columns[None, :]).astype(jnp.float32)
    weights = (jax.nn.sigmoid(logits) - match).astype(jnp.bfloat16)
    running = jnp.dot(weights, all_texts, preferred_element_type=jnp.float32)
    grad_unit = swapped_sum(logit_scale * running, "tensor")
    grad_mixed = (
        grad_unit - image_unit * jnp.sum(image_unit * grad_unit, axis=1, keepdims=True)
    ) / row_norm
    grad_b = grad_mixed.astype(jnp.bfloat16)
    grad_own, grad_other = parity_split(grad_b, core, chips)
    grad_hidden = jnp.einsum(
        "rd,df->rf", grad_own, own_out, preferred_element_type=jnp.float32
    ) + jnp.einsum("rd,df->rf", grad_other, other_out, preferred_element_type=jnp.float32)
    _, gelu_back = jax.vjp(gelu_tanh, pre_act)
    grad_pre = gelu_back(grad_hidden)[0].astype(jnp.bfloat16)
    unit_parts = jnp.concatenate(
        [
            jnp.einsum("rf,df->rd", grad_pre, own_in, preferred_element_type=jnp.float32),
            jnp.einsum("rf,df->rd", grad_pre, other_in, preferred_element_type=jnp.float32),
        ],
        axis=1,
    )
    unit_sum = swapped_sum(unit_parts, "tensor")
    grad_unit_in = parity_join(unit_sum[:, :half], unit_sum[:, half:], core, chips)
    scaled = grad_unit_in * ln_gain
    grad_rows = inv_std * (
        scaled
        - jnp.mean(scaled, axis=1, keepdims=True)
        - normal_rows * jnp.mean(scaled * normal_rows, axis=1, keepdims=True)
    )
    grad_pooled = (grad_mixed + grad_rows)[None]

    width = grad_pre.shape[1]
    terms_own = jnp.concatenate(
        [
            jnp.einsum("rd,rf->df", unit_own, grad_pre, preferred_element_type=jnp.float32),
            jnp.einsum("rd,rf->df", grad_own, hidden, preferred_element_type=jnp.float32),
        ],
        axis=1,
    )
    terms_other = jnp.concatenate(
        [
            jnp.einsum("rd,rf->df", unit_other, grad_pre, preferred_element_type=jnp.float32),
            jnp.einsum("rd,rf->df", grad_other, hidden, preferred_element_type=jnp.float32),
        ],
        axis=1,
    )
    terms_chip = terms_own.astype(jnp.bfloat16).astype(jnp.float32) + core_swap(
        terms_other.astype(jnp.bfloat16)
    ).astype(jnp.float32)
    terms_part = lax.psum_scatter(
        terms_chip.astype(jnp.bfloat16), "z", scatter_dimension=0, tiled=True
    )
    (total,) = doubling_sum([terms_part], "dp")
    grad_in = total[:, :width]
    grad_out = total[:, width:].T
    return (grad_pooled, grad_in, grad_out)


def solution(mesh):
    fsdp = mesh.shape["fsdp"]
    chip_mesh = Mesh(
        mesh.devices.reshape(mesh.shape["dp"], fsdp // 2, 2, mesh.shape["tensor"]),
        ("dp", "z", "core", "tensor"),
    )
    placed = (
        P("dp", ("z", "core"), None),
        P(),
        P(("z", "core"), "tensor"),
        P("tensor", ("z", "core")),
        P("dp", ("z", "core", "tensor"), None),
    )
    return jax.shard_map(
        layer,
        mesh=chip_mesh,
        in_specs=placed,
        out_specs=(
            P("dp", ("z", "core"), None),
            P(("z", "core"), "tensor"),
            P("tensor", ("z", "core")),
        ),
        check_vma=False,
    )
```

```python
import jax
import jax.numpy as jnp
from jax import lax
from jax.sharding import Mesh
from jax.sharding import PartitionSpec as P


ln_eps = 1e-06
norm_eps = 1e-06
logit_scale = 10.0
logit_bias = -2.0


def passed_along(block, axis, distance):
    devices = range(lax.axis_size(axis))
    route = [((i - distance) % len(devices), i) for i in devices]
    return lax.ppermute(block, axis, route)


def core_swap(block):
    return lax.ppermute(block, "core", [(0, 1), (1, 0)])


def swapped_sum(partial, axis):
    mine = partial.astype(jnp.bfloat16)
    other = lax.ppermute(mine, axis, [(0, 1), (1, 0)])
    return mine.astype(jnp.float32) + other.astype(jnp.float32)


def doubling_sum(parts, axis):
    size = lax.axis_size(axis)
    mine = [p.astype(jnp.bfloat16) for p in parts]
    totals = None
    bit = 1
    while bit < size:
        route = [(i, i ^ bit) for i in range(size)]
        others = [lax.ppermute(m, axis, route) for m in mine]
        totals = [m.astype(jnp.float32) + o.astype(jnp.float32) for m, o in zip(mine, others)]
        mine = [t.astype(jnp.bfloat16) for t in totals]
        bit *= 2
    return totals


def parity_split(values, core, chips):
    lead = values.shape[:-1]
    blocks = values.reshape(lead + (chips, 2, values.shape[-1] // (2 * chips)))
    axis = blocks.ndim - 2
    own = lax.dynamic_index_in_dim(blocks, core, axis=axis, keepdims=False)
    other = lax.dynamic_index_in_dim(blocks, 1 - core, axis=axis, keepdims=False)
    half = lead + (values.shape[-1] // 2,)
    return own.reshape(half), other.reshape(half)


def parity_join(own, other, core, chips):
    lead = own.shape[:-1]
    shape = lead + (chips, 1, own.shape[-1] // chips)
    own = own.reshape(shape)
    other = other.reshape(shape)
    even = jnp.where(core == 0, own, other)
    odd = jnp.where(core == 0, other, own)
    return jnp.concatenate([even, odd], axis=-2).reshape(lead + (2 * own.shape[-1] * chips,))


def gelu_tanh(values):
    return jax.nn.gelu(values, approximate=True)


def unit_rows(values):
    return values / jnp.sqrt(jnp.sum(values * values, axis=-1, keepdims=True) + norm_eps)


def layer(pooled, ln_gain, w_in, w_out, texts):
    rows = pooled[0].astype(jnp.float32)
    images = rows.shape[0]
    chip = lax.axis_index("z")
    chips = lax.axis_size("z")
    core = lax.axis_index("core")
    block_index = chip * 2 + core

    text_b = unit_rows(texts[0].astype(jnp.float32)).astype(jnp.bfloat16)
    block_rows = text_b.shape[0]
    half_index = lax.axis_index("tensor")
    within = jnp.arange(block_rows, dtype=jnp.int32)

    def block_columns(source_chip, parity, half):
        return (source_chip * 2 + parity) * images + half * block_rows + within

    blocks = [text_b]
    sources = [chip]
    ahead = text_b
    for step in range(1, chips // 2 + 1):
        ahead = passed_along(ahead, "z", 1)
        blocks.append(ahead)
        sources.append((chip - step) % chips)
    behind = text_b
    for step in range(1, (chips - 1) // 2 + 1):
        behind = passed_along(behind, "z", -1)
        blocks.append(behind)
        sources.append((chip + step) % chips)
    own_texts = jnp.concatenate(blocks, axis=0)
    core_texts = jnp.concatenate([own_texts, core_swap(own_texts)], axis=0)
    all_texts = jnp.concatenate(
        [core_texts, lax.ppermute(core_texts, "tensor", [(0, 1), (1, 0)])], axis=0
    )
    columns = jnp.concatenate(
        [block_columns(s, core, half_index) for s in sources]
        + [block_columns(s, 1 - core, half_index) for s in sources]
        + [block_columns(s, core, 1 - half_index) for s in sources]
        + [block_columns(s, 1 - core, 1 - half_index) for s in sources],
        axis=0,
    )

    stacked = jnp.stack([w_in, w_out.T])
    own_w = lax.all_gather(stacked, "z", axis=1, tiled=True)
    other_w = core_swap(own_w)
    own_in, own_out = own_w[0], own_w[1]
    other_in, other_out = other_w[0], other_w[1]

    row_mean = jnp.mean(rows, axis=1, keepdims=True)
    centred = rows - row_mean
    inv_std = lax.rsqrt(jnp.mean(centred * centred, axis=1, keepdims=True) + ln_eps)
    normal_rows = centred * inv_std
    unit_in = (normal_rows * ln_gain).astype(jnp.bfloat16)
    unit_own, unit_other = parity_split(unit_in, core, chips)
    pre_act = jnp.dot(unit_own, own_in, preferred_element_type=jnp.float32) + jnp.dot(
        unit_other, other_in, preferred_element_type=jnp.float32
    )
    hidden = gelu_tanh(pre_act).astype(jnp.bfloat16)
    mix_parts = jnp.concatenate(
        [
            jnp.einsum("rf,df->rd", hidden, own_out, preferred_element_type=jnp.float32),
            jnp.einsum("rf,df->rd", hidden, other_out, preferred_element_type=jnp.float32),
        ],
        axis=1,
    )
    mix_sum = swapped_sum(mix_parts, "tensor")
    half = mix_sum.shape[1] // 2
    mixed = rows + parity_join(mix_sum[:, :half], mix_sum[:, half:], core, chips)
    row_norm = jnp.sqrt(jnp.sum(mixed * mixed, axis=1, keepdims=True) + norm_eps)
    image_unit = mixed / row_norm
    image_b = image_unit.astype(jnp.bfloat16)
    image_places = block_index * images + jnp.arange(images, dtype=jnp.int32)

    logits = (
        logit_scale
        * jnp.einsum("rd,cd->rc", image_b, all_texts, preferred_element_type=jnp.float32)
        + logit_bias
    )
    match = (image_places[:, None] == columns[None, :]).astype(jnp.float32)
    weights = (jax.nn.sigmoid(logits) - match).astype(jnp.bfloat16)
    running = jnp.dot(weights, all_texts, preferred_element_type=jnp.float32)
    grad_unit = logit_scale * running
    grad_mixed = (
        grad_unit - image_unit * jnp.sum(image_unit * grad_unit, axis=1, keepdims=True)
    ) / row_norm
    grad_b = grad_mixed.astype(jnp.bfloat16)
    grad_own, grad_other = parity_split(grad_b, core, chips)
    grad_hidden = jnp.einsum(
        "rd,df->rf", grad_own, own_out, preferred_element_type=jnp.float32
    ) + jnp.einsum("rd,df->rf", grad_other, other_out, preferred_element_type=jnp.float32)
    _, gelu_back = jax.vjp(gelu_tanh, pre_act)
    grad_pre = gelu_back(grad_hidden)[0].astype(jnp.bfloat16)
    unit_parts = jnp.concatenate(
        [
            jnp.einsum("rf,df->rd", grad_pre, own_in, preferred_element_type=jnp.float32),
            jnp.einsum("rf,df->rd", grad_pre, other_in, preferred_element_type=jnp.float32),
        ],
        axis=1,
    )
    unit_sum = swapped_sum(unit_parts, "tensor")
    grad_unit_in = parity_join(unit_sum[:, :half], unit_sum[:, half:], core, chips)
    scaled = grad_unit_in * ln_gain
    grad_rows = inv_std * (
        scaled
        - jnp.mean(scaled, axis=1, keepdims=True)
        - normal_rows * jnp.mean(scaled * normal_rows, axis=1, keepdims=True)
    )
    grad_pooled = (grad_mixed + grad_rows)[None]

    width = grad_pre.shape[1]
    terms_own = jnp.concatenate(
        [
            jnp.einsum("rd,rf->df", unit_own, grad_pre, preferred_element_type=jnp.float32),
            jnp.einsum("rd,rf->df", grad_own, hidden, preferred_element_type=jnp.float32),
        ],
        axis=1,
    )
    terms_other = jnp.concatenate(
        [
            jnp.einsum("rd,rf->df", unit_other, grad_pre, preferred_element_type=jnp.float32),
            jnp.einsum("rd,rf->df", grad_other, hidden, preferred_element_type=jnp.float32),
        ],
        axis=1,
    )
    terms_chip = terms_own.astype(jnp.bfloat16).astype(jnp.float32) + core_swap(
        terms_other.astype(jnp.bfloat16)
    ).astype(jnp.float32)
    terms_part = lax.psum_scatter(
        terms_chip.astype(jnp.bfloat16), "z", scatter_dimension=0, tiled=True
    )
    (total,) = doubling_sum([terms_part], "dp")
    grad_in = total[:, :width]
    grad_out = total[:, width:].T
    return (grad_pooled, grad_in, grad_out)


def solution(mesh):
    fsdp = mesh.shape["fsdp"]
    chip_mesh = Mesh(
        mesh.devices.reshape(mesh.shape["dp"], fsdp // 2, 2, mesh.shape["tensor"]),
        ("dp", "z", "core", "tensor"),
    )
    placed = (
        P("dp", ("z", "core"), None),
        P(),
        P(("z", "core"), "tensor"),
        P("tensor", ("z", "core")),
        P("dp", ("z", "core", "tensor"), None),
    )
    return jax.shard_map(
        layer,
        mesh=chip_mesh,
        in_specs=placed,
        out_specs=(
            P("dp", ("z", "core"), None),
            P(("z", "core"), "tensor"),
            P("tensor", ("z", "core")),
        ),
        check_vma=False,
    )
```

```python
import jax
import jax.numpy as jnp
from jax import lax
from jax.sharding import Mesh
from jax.sharding import PartitionSpec as P


ln_eps = 1e-06
norm_eps = 1e-06
logit_scale = 10.0
logit_bias = -2.0


def passed_along(block, axis, distance):
    devices = range(lax.axis_size(axis))
    route = [((i - distance) % len(devices), i) for i in devices]
    return lax.ppermute(block, axis, route)


def core_swap(block):
    return lax.ppermute(block, "core", [(0, 1), (1, 0)])


def swapped_sum(partial, axis):
    mine = partial.astype(jnp.bfloat16)
    other = lax.ppermute(mine, axis, [(0, 1), (1, 0)])
    return mine.astype(jnp.float32) + other.astype(jnp.float32)


def halving_sum(values, axis):
    size = lax.axis_size(axis)
    index = lax.axis_index(axis)
    bits = []
    bit = 1
    while bit < size:
        bits.append(bit)
        bit *= 2
    part = values.reshape(-1).astype(jnp.float32)
    for bit in bits:
        half = part.shape[0] // 2
        upper = (index // bit) % 2 == 1
        keep = jnp.where(upper, part[half:], part[:half])
        send = jnp.where(upper, part[:half], part[half:])
        route = [(i, i ^ bit) for i in range(size)]
        got = lax.ppermute(send.astype(jnp.bfloat16), axis, route)
        part = keep.astype(jnp.bfloat16).astype(jnp.float32) + got.astype(jnp.float32)
    held = part.astype(jnp.bfloat16)
    for bit in reversed(bits):
        upper = (index // bit) % 2 == 1
        route = [(i, i ^ bit) for i in range(size)]
        got = lax.ppermute(held, axis, route)
        held = jnp.where(
            upper, jnp.concatenate([got, held]), jnp.concatenate([held, got])
        )
    return held.reshape(values.shape).astype(jnp.float32)


def parity_split(values, core, chips):
    lead = values.shape[:-1]
    blocks = values.reshape(lead + (chips, 2, values.shape[-1] // (2 * chips)))
    axis = blocks.ndim - 2
    own = lax.dynamic_index_in_dim(blocks, core, axis=axis, keepdims=False)
    other = lax.dynamic_index_in_dim(blocks, 1 - core, axis=axis, keepdims=False)
    half = lead + (values.shape[-1] // 2,)
    return own.reshape(half), other.reshape(half)


def parity_join(own, other, core, chips):
    lead = own.shape[:-1]
    shape = lead + (chips, 1, own.shape[-1] // chips)
    own = own.reshape(shape)
    other = other.reshape(shape)
    even = jnp.where(core == 0, own, other)
    odd = jnp.where(core == 0, other, own)
    return jnp.concatenate([even, odd], axis=-2).reshape(lead + (2 * own.shape[-1] * chips,))


def gelu_tanh(values):
    return jax.nn.gelu(values, approximate=True)


def unit_rows(values):
    return values / jnp.sqrt(jnp.sum(values * values, axis=-1, keepdims=True) + norm_eps)


def layer(pooled, ln_gain, w_in, w_out, texts):
    rows = pooled[0].astype(jnp.float32)
    images = rows.shape[0]
    chip = lax.axis_index("z")
    chips = lax.axis_size("z")
    core = lax.axis_index("core")
    block_index = chip * 2 + core

    text_b = unit_rows(texts[0].astype(jnp.float32)).astype(jnp.bfloat16)
    block_rows = text_b.shape[0]
    half_index = lax.axis_index("tensor")
    within = jnp.arange(block_rows, dtype=jnp.int32)

    def block_columns(source_chip, parity, half):
        return (source_chip * 2 + parity) * images + half * block_rows + within

    blocks = [text_b]
    sources = [chip]
    ahead = text_b
    for step in range(1, chips // 2 + 1):
        ahead = passed_along(ahead, "z", 1)
        blocks.append(ahead)
        sources.append((chip - step) % chips)
    behind = text_b
    for step in range(1, (chips - 1) // 2 + 1):
        behind = passed_along(behind, "z", -1)
        blocks.append(behind)
        sources.append((chip + step) % chips)
    own_texts = jnp.concatenate(blocks, axis=0)
    core_texts = jnp.concatenate([own_texts, core_swap(own_texts)], axis=0)
    all_texts = core_texts
    columns = jnp.concatenate(
        [block_columns(s, core, half_index) for s in sources]
        + [block_columns(s, 1 - core, half_index) for s in sources],
        axis=0,
    )

    stacked = jnp.stack([w_in, w_out.T])
    own_w = lax.all_gather(stacked, "z", axis=1, tiled=True)
    other_w = core_swap(own_w)
    own_in, own_out = own_w[0], own_w[1]
    other_in, other_out = other_w[0], other_w[1]

    row_mean = jnp.mean(rows, axis=1, keepdims=True)
    centred = rows - row_mean
    inv_std = lax.rsqrt(jnp.mean(centred * centred, axis=1, keepdims=True) + ln_eps)
    normal_rows = centred * inv_std
    unit_in = (normal_rows * ln_gain).astype(jnp.bfloat16)
    unit_own, unit_other = parity_split(unit_in, core, chips)
    pre_act = jnp.dot(unit_own, own_in, preferred_element_type=jnp.float32) + jnp.dot(
        unit_other, other_in, preferred_element_type=jnp.float32
    )
    hidden = gelu_tanh(pre_act).astype(jnp.bfloat16)
    mix_parts = jnp.concatenate(
        [
            jnp.einsum("rf,df->rd", hidden, own_out, preferred_element_type=jnp.float32),
            jnp.einsum("rf,df->rd", hidden, other_out, preferred_element_type=jnp.float32),
        ],
        axis=1,
    )
    mix_sum = swapped_sum(mix_parts, "tensor")
    half = mix_sum.shape[1] // 2
    mixed = rows + parity_join(mix_sum[:, :half], mix_sum[:, half:], core, chips)
    row_norm = jnp.sqrt(jnp.sum(mixed * mixed, axis=1, keepdims=True) + norm_eps)
    image_unit = mixed / row_norm
    image_b = image_unit.astype(jnp.bfloat16)
    image_places = block_index * images + jnp.arange(images, dtype=jnp.int32)

    logits = (
        logit_scale
        * jnp.einsum("rd,cd->rc", image_b, all_texts, preferred_element_type=jnp.float32)
        + logit_bias
    )
    match = (image_places[:, None] == columns[None, :]).astype(jnp.float32)
    weights = (jax.nn.sigmoid(logits) - match).astype(jnp.bfloat16)
    running = jnp.dot(weights, all_texts, preferred_element_type=jnp.float32)
    grad_unit = swapped_sum(logit_scale * running, "tensor")
    grad_mixed = (
        grad_unit - image_unit * jnp.sum(image_unit * grad_unit, axis=1, keepdims=True)
    ) / row_norm
    grad_b = grad_mixed.astype(jnp.bfloat16)
    grad_own, grad_other = parity_split(grad_b, core, chips)
    grad_hidden = jnp.einsum(
        "rd,df->rf", grad_own, own_out, preferred_element_type=jnp.float32
    ) + jnp.einsum("rd,df->rf", grad_other, other_out, preferred_element_type=jnp.float32)
    _, gelu_back = jax.vjp(gelu_tanh, pre_act)
    grad_pre = gelu_back(grad_hidden)[0].astype(jnp.bfloat16)
    unit_parts = jnp.concatenate(
        [
            jnp.einsum("rf,df->rd", grad_pre, own_in, preferred_element_type=jnp.float32),
            jnp.einsum("rf,df->rd", grad_pre, other_in, preferred_element_type=jnp.float32),
        ],
        axis=1,
    )
    unit_sum = swapped_sum(unit_parts, "tensor")
    grad_unit_in = parity_join(unit_sum[:, :half], unit_sum[:, half:], core, chips)
    scaled = grad_unit_in * ln_gain
    grad_rows = inv_std * (
        scaled
        - jnp.mean(scaled, axis=1, keepdims=True)
        - normal_rows * jnp.mean(scaled * normal_rows, axis=1, keepdims=True)
    )
    grad_pooled = (grad_mixed + grad_rows)[None]

    width = grad_pre.shape[1]
    terms_own = jnp.concatenate(
        [
            jnp.einsum("rd,rf->df", unit_own, grad_pre, preferred_element_type=jnp.float32),
            jnp.einsum("rd,rf->df", grad_own, hidden, preferred_element_type=jnp.float32),
        ],
        axis=1,
    )
    terms_other = jnp.concatenate(
        [
            jnp.einsum("rd,rf->df", unit_other, grad_pre, preferred_element_type=jnp.float32),
            jnp.einsum("rd,rf->df", grad_other, hidden, preferred_element_type=jnp.float32),
        ],
        axis=1,
    )
    terms_chip = terms_own.astype(jnp.bfloat16).astype(jnp.float32) + core_swap(
        terms_other.astype(jnp.bfloat16)
    ).astype(jnp.float32)
    terms_part = lax.psum_scatter(
        terms_chip.astype(jnp.bfloat16), "z", scatter_dimension=0, tiled=True
    )
    total = halving_sum(terms_part, "dp")
    grad_in = total[:, :width]
    grad_out = total[:, width:].T
    return (grad_pooled, grad_in, grad_out)


def solution(mesh):
    fsdp = mesh.shape["fsdp"]
    chip_mesh = Mesh(
        mesh.devices.reshape(mesh.shape["dp"], fsdp // 2, 2, mesh.shape["tensor"]),
        ("dp", "z", "core", "tensor"),
    )
    placed = (
        P("dp", ("z", "core"), None),
        P(),
        P(("z", "core"), "tensor"),
        P("tensor", ("z", "core")),
        P("dp", ("z", "core", "tensor"), None),
    )
    return jax.shard_map(
        layer,
        mesh=chip_mesh,
        in_specs=placed,
        out_specs=(
            P("dp", ("z", "core"), None),
            P(("z", "core"), "tensor"),
            P("tensor", ("z", "core")),
        ),
        check_vma=False,
    )
```

```python
import jax
import jax.numpy as jnp
from jax import lax
from jax.sharding import Mesh
from jax.sharding import PartitionSpec as P


ln_eps = 1e-06
norm_eps = 1e-06
logit_scale = 10.0
logit_bias = -2.0


def passed_along(block, axis, distance):
    devices = range(lax.axis_size(axis))
    route = [((i - distance) % len(devices), i) for i in devices]
    return lax.ppermute(block, axis, route)


def core_swap(block):
    return lax.ppermute(block, "core", [(0, 1), (1, 0)])


def swapped_sum(partial, axis):
    mine = partial.astype(jnp.bfloat16)
    other = lax.ppermute(mine, axis, [(0, 1), (1, 0)])
    return mine.astype(jnp.float32) + other.astype(jnp.float32)


def doubling_sum(parts, axis):
    size = lax.axis_size(axis)
    mine = [p.astype(jnp.bfloat16) for p in parts]
    totals = None
    bit = 1
    while bit < size:
        route = [(i, i ^ bit) for i in range(size)]
        others = [lax.ppermute(m, axis, route) for m in mine]
        totals = [m.astype(jnp.float32) + o.astype(jnp.float32) for m, o in zip(mine, others)]
        mine = [t.astype(jnp.bfloat16) for t in totals]
        bit *= 2
    return totals


def parity_split(values, core, chips):
    lead = values.shape[:-1]
    blocks = values.reshape(lead + (chips, 2, values.shape[-1] // (2 * chips)))
    axis = blocks.ndim - 2
    own = lax.dynamic_index_in_dim(blocks, core, axis=axis, keepdims=False)
    other = lax.dynamic_index_in_dim(blocks, 1 - core, axis=axis, keepdims=False)
    half = lead + (values.shape[-1] // 2,)
    return own.reshape(half), other.reshape(half)


def parity_join(own, other, core, chips):
    lead = own.shape[:-1]
    shape = lead + (chips, 1, own.shape[-1] // chips)
    own = own.reshape(shape)
    other = other.reshape(shape)
    even = jnp.where(core == 0, own, other)
    odd = jnp.where(core == 0, other, own)
    return jnp.concatenate([even, odd], axis=-2).reshape(lead + (2 * own.shape[-1] * chips,))


def gelu_tanh(values):
    return jax.nn.gelu(values, approximate=True)


def unit_rows(values):
    return values / jnp.sqrt(jnp.sum(values * values, axis=-1, keepdims=True) + norm_eps)


def layer(pooled, ln_gain, w_in, w_out, texts):
    rows = pooled[0].astype(jnp.float32)
    images = rows.shape[0]
    chip = lax.axis_index("z")
    chips = lax.axis_size("z")
    core = lax.axis_index("core")
    block_index = chip * 2 + core

    text_b = unit_rows(texts[0].astype(jnp.float32)).astype(jnp.bfloat16)
    block_rows = text_b.shape[0]
    half_index = lax.axis_index("tensor")
    within = jnp.arange(block_rows, dtype=jnp.int32)

    def block_columns(source_chip, parity, half):
        return (source_chip * 2 + parity) * images + half * block_rows + within

    blocks = [text_b]
    sources = [chip]
    ahead = text_b
    for step in range(1, chips // 2 + 1):
        ahead = passed_along(ahead, "z", 1)
        blocks.append(ahead)
        sources.append((chip - step) % chips)
    behind = text_b
    for step in range(1, (chips - 1) // 2 + 1):
        behind = passed_along(behind, "z", -1)
        blocks.append(behind)
        sources.append((chip + step) % chips)
    own_texts = jnp.concatenate(blocks, axis=0)
    core_texts = jnp.concatenate([own_texts, core_swap(own_texts)], axis=0)
    all_texts = core_texts
    columns = jnp.concatenate(
        [block_columns(s, core, half_index) for s in sources]
        + [block_columns(s, 1 - core, half_index) for s in sources],
        axis=0,
    )

    stacked = jnp.stack([w_in, w_out.T])
    own_w = lax.all_gather(stacked, "z", axis=1, tiled=True)
    other_w = core_swap(own_w)
    own_in, own_out = own_w[0], own_w[1]
    other_in, other_out = other_w[0], other_w[1]

    row_mean = jnp.mean(rows, axis=1, keepdims=True)
    centred = rows - row_mean
    inv_std = lax.rsqrt(jnp.mean(centred * centred, axis=1, keepdims=True) + ln_eps)
    normal_rows = centred * inv_std
    unit_in = (normal_rows * ln_gain).astype(jnp.bfloat16)
    unit_own, unit_other = parity_split(unit_in, core, chips)

    pre_act = jnp.dot(unit_own, own_in, preferred_element_type=jnp.float32) + jnp.dot(
        unit_other, other_in, preferred_element_type=jnp.float32
    )
    hidden = gelu_tanh(pre_act).astype(jnp.bfloat16)
    mix_parts = jnp.concatenate(
        [
            jnp.einsum("rf,df->rd", hidden, own_out, preferred_element_type=jnp.float32),
            jnp.einsum("rf,df->rd", hidden, other_out, preferred_element_type=jnp.float32),
        ],
        axis=1,
    )
    mix_sum = swapped_sum(mix_parts, "tensor")
    half = mix_sum.shape[1] // 2
    mixed = rows + parity_join(mix_sum[:, :half], mix_sum[:, half:], core, chips)
    row_norm = jnp.sqrt(jnp.sum(mixed * mixed, axis=1, keepdims=True) + norm_eps)
    image_unit = mixed / row_norm
    image_b = image_unit.astype(jnp.bfloat16)
    image_places = block_index * images + jnp.arange(images, dtype=jnp.int32)

    logits = (
        logit_scale
        * jnp.einsum("rd,cd->rc", image_b, all_texts, preferred_element_type=jnp.float32)
        + logit_bias
    )
    match = (image_places[:, None] == columns[None, :]).astype(jnp.float32)
    weights = (jax.nn.sigmoid(logits) - match).astype(jnp.bfloat16)
    running = jnp.dot(weights, all_texts, preferred_element_type=jnp.float32)
    grad_unit = swapped_sum(logit_scale * running, "tensor")
    grad_mixed = (
        grad_unit - image_unit * jnp.sum(image_unit * grad_unit, axis=1, keepdims=True)
    ) / row_norm
    grad_b = grad_mixed.astype(jnp.bfloat16)
    grad_own, grad_other = parity_split(grad_b, core, chips)
    grad_hidden = jnp.einsum(
        "rd,df->rf", grad_own, own_out, preferred_element_type=jnp.float32
    ) + jnp.einsum("rd,df->rf", grad_other, other_out, preferred_element_type=jnp.float32)
    _, gelu_back = jax.vjp(gelu_tanh, pre_act)
    grad_pre = gelu_back(grad_hidden)[0].astype(jnp.bfloat16)
    unit_parts = jnp.concatenate(
        [
            jnp.einsum("rf,df->rd", grad_pre, own_in, preferred_element_type=jnp.float32),
            jnp.einsum("rf,df->rd", grad_pre, other_in, preferred_element_type=jnp.float32),
        ],
        axis=1,
    )
    unit_sum = swapped_sum(unit_parts, "tensor")
    grad_unit_in = parity_join(unit_sum[:, :half], unit_sum[:, half:], core, chips)
    scaled = grad_unit_in * ln_gain
    grad_rows = inv_std * (
        scaled
        - jnp.mean(scaled, axis=1, keepdims=True)
        - normal_rows * jnp.mean(scaled * normal_rows, axis=1, keepdims=True)
    )
    grad_pooled = (grad_mixed + grad_rows)[None]

    width = grad_pre.shape[1]
    terms_own = jnp.concatenate(
        [
            jnp.einsum("rd,rf->df", unit_own, grad_pre, preferred_element_type=jnp.float32),
            jnp.einsum("rd,rf->df", grad_own, hidden, preferred_element_type=jnp.float32),
        ],
        axis=1,
    )
    terms_other = jnp.concatenate(
        [
            jnp.einsum("rd,rf->df", unit_other, grad_pre, preferred_element_type=jnp.float32),
            jnp.einsum("rd,rf->df", grad_other, hidden, preferred_element_type=jnp.float32),
        ],
        axis=1,
    )
    terms_chip = terms_own.astype(jnp.bfloat16).astype(jnp.float32) + core_swap(
        terms_other.astype(jnp.bfloat16)
    ).astype(jnp.float32)
    terms_part = lax.psum_scatter(
        terms_chip.astype(jnp.bfloat16), "z", scatter_dimension=0, tiled=True
    )
    (total,) = doubling_sum([terms_part], "dp")
    grad_in = total[:, :width]
    grad_out = total[:, width:].T
    return (grad_pooled, grad_in, grad_out)


def solution(mesh):
    fsdp = mesh.shape["fsdp"]
    chip_mesh = Mesh(
        mesh.devices.reshape(mesh.shape["dp"], fsdp // 2, 2, mesh.shape["tensor"]),
        ("dp", "z", "core", "tensor"),
    )
    placed = (
        P("dp", ("z", "core"), None),
        P(),
        P(("z", "core"), "tensor"),
        P("tensor", ("z", "core")),
        P("dp", ("z", "core", "tensor"), None),
    )
    return jax.shard_map(
        layer,
        mesh=chip_mesh,
        in_specs=placed,
        out_specs=(
            P("dp", ("z", "core"), None),
            P(("z", "core"), "tensor"),
            P("tensor", ("z", "core")),
        ),
        check_vma=False,
    )
```

```python
import jax
import jax.numpy as jnp
from jax import lax
from jax.sharding import Mesh
from jax.sharding import PartitionSpec as P


ln_eps = 1e-06
norm_eps = 1e-06
logit_scale = 10.0
logit_bias = -2.0


def passed_along(block, axis, distance):
    devices = range(lax.axis_size(axis))
    route = [((i - distance) % len(devices), i) for i in devices]
    return lax.ppermute(block, axis, route)


def core_swap(block):
    return lax.ppermute(block, "core", [(0, 1), (1, 0)])


def swapped_sum(partial, axis):
    mine = partial.astype(jnp.bfloat16)
    other = lax.ppermute(mine, axis, [(0, 1), (1, 0)])
    return mine.astype(jnp.float32) + other.astype(jnp.float32)


def ring_dp_sum(values):
    size = lax.axis_size("dp")
    pair = [(i, i ^ 1) for i in range(size)]
    mine = values.astype(jnp.bfloat16)
    paired = (
        mine.astype(jnp.float32) + lax.ppermute(mine, "dp", pair).astype(jnp.float32)
    ).astype(jnp.bfloat16)
    left = lax.ppermute(paired, "dp", [(i, (i + 2) % size) for i in range(size)])
    right = lax.ppermute(paired, "dp", [(i, (i - 2) % size) for i in range(size)])
    across = lax.ppermute(right, "dp", [(i, (i - 2) % size) for i in range(size)])
    ring = size // 2
    place = lax.axis_index("dp") // 2
    by_offset = [paired, right, across, left]
    slots = []
    for p in range(ring):
        offset = (p - place) % ring
        value = by_offset[0]
        for k in range(1, ring):
            value = jnp.where(offset == k, by_offset[k], value)
        slots.append(value.astype(jnp.float32))
    return (slots[0] + slots[1]) + (slots[2] + slots[3])


def parity_split(values, core, chips):
    lead = values.shape[:-1]
    blocks = values.reshape(lead + (chips, 2, values.shape[-1] // (2 * chips)))
    axis = blocks.ndim - 2
    own = lax.dynamic_index_in_dim(blocks, core, axis=axis, keepdims=False)
    other = lax.dynamic_index_in_dim(blocks, 1 - core, axis=axis, keepdims=False)
    half = lead + (values.shape[-1] // 2,)
    return own.reshape(half), other.reshape(half)


def parity_join(own, other, core, chips):
    lead = own.shape[:-1]
    shape = lead + (chips, 1, own.shape[-1] // chips)
    own = own.reshape(shape)
    other = other.reshape(shape)
    even = jnp.where(core == 0, own, other)
    odd = jnp.where(core == 0, other, own)
    return jnp.concatenate([even, odd], axis=-2).reshape(lead + (2 * own.shape[-1] * chips,))


def gelu_tanh(values):
    return jax.nn.gelu(values, approximate=True)


def unit_rows(values):
    return values / jnp.sqrt(jnp.sum(values * values, axis=-1, keepdims=True) + norm_eps)


def layer(pooled, ln_gain, w_in, w_out, texts):
    rows = pooled[0].astype(jnp.float32)
    images = rows.shape[0]
    chip = lax.axis_index("z")
    chips = lax.axis_size("z")
    core = lax.axis_index("core")
    block_index = chip * 2 + core

    text_b = unit_rows(texts[0].astype(jnp.float32)).astype(jnp.bfloat16)
    block_rows = text_b.shape[0]
    half_index = lax.axis_index("tensor")
    within = jnp.arange(block_rows, dtype=jnp.int32)

    def block_columns(source_chip, parity, half):
        return (source_chip * 2 + parity) * images + half * block_rows + within

    blocks = [text_b]
    sources = [chip]
    ahead = text_b
    for step in range(1, chips // 2 + 1):
        ahead = passed_along(ahead, "z", 1)
        blocks.append(ahead)
        sources.append((chip - step) % chips)
    behind = text_b
    for step in range(1, (chips - 1) // 2 + 1):
        behind = passed_along(behind, "z", -1)
        blocks.append(behind)
        sources.append((chip + step) % chips)
    own_texts = jnp.concatenate(blocks, axis=0)
    core_texts = jnp.concatenate([own_texts, core_swap(own_texts)], axis=0)
    all_texts = core_texts
    columns = jnp.concatenate(
        [block_columns(s, core, half_index) for s in sources]
        + [block_columns(s, 1 - core, half_index) for s in sources],
        axis=0,
    )

    stacked = jnp.stack([w_in, w_out.T])
    own_w = lax.all_gather(stacked, "z", axis=1, tiled=True)
    other_w = core_swap(own_w)
    own_in, own_out = own_w[0], own_w[1]
    other_in, other_out = other_w[0], other_w[1]

    row_mean = jnp.mean(rows, axis=1, keepdims=True)
    centred = rows - row_mean
    inv_std = lax.rsqrt(jnp.mean(centred * centred, axis=1, keepdims=True) + ln_eps)
    normal_rows = centred * inv_std
    unit_in = (normal_rows * ln_gain).astype(jnp.bfloat16)
    unit_own, unit_other = parity_split(unit_in, core, chips)
    pre_act = jnp.dot(unit_own, own_in, preferred_element_type=jnp.float32) + jnp.dot(
        unit_other, other_in, preferred_element_type=jnp.float32
    )
    hidden = gelu_tanh(pre_act).astype(jnp.bfloat16)
    mix_parts = jnp.concatenate(
        [
            jnp.einsum("rf,df->rd", hidden, own_out, preferred_element_type=jnp.float32),
            jnp.einsum("rf,df->rd", hidden, other_out, preferred_element_type=jnp.float32),
        ],
        axis=1,
    )
    mix_sum = swapped_sum(mix_parts, "tensor")
    half = mix_sum.shape[1] // 2
    mixed = rows + parity_join(mix_sum[:, :half], mix_sum[:, half:], core, chips)
    row_norm = jnp.sqrt(jnp.sum(mixed * mixed, axis=1, keepdims=True) + norm_eps)
    image_unit = mixed / row_norm
    image_b = image_unit.astype(jnp.bfloat16)
    image_places = block_index * images + jnp.arange(images, dtype=jnp.int32)

    logits = (
        logit_scale
        * jnp.einsum("rd,cd->rc", image_b, all_texts, preferred_element_type=jnp.float32)
        + logit_bias
    )
    match = (image_places[:, None] == columns[None, :]).astype(jnp.float32)
    weights = (jax.nn.sigmoid(logits) - match).astype(jnp.bfloat16)
    running = jnp.dot(weights, all_texts, preferred_element_type=jnp.float32)
    grad_unit = swapped_sum(logit_scale * running, "tensor")
    grad_mixed = (
        grad_unit - image_unit * jnp.sum(image_unit * grad_unit, axis=1, keepdims=True)
    ) / row_norm
    grad_b = grad_mixed.astype(jnp.bfloat16)
    grad_own, grad_other = parity_split(grad_b, core, chips)
    grad_hidden = jnp.einsum(
        "rd,df->rf", grad_own, own_out, preferred_element_type=jnp.float32
    ) + jnp.einsum("rd,df->rf", grad_other, other_out, preferred_element_type=jnp.float32)
    _, gelu_back = jax.vjp(gelu_tanh, pre_act)
    grad_pre = gelu_back(grad_hidden)[0].astype(jnp.bfloat16)
    unit_parts = jnp.concatenate(
        [
            jnp.einsum("rf,df->rd", grad_pre, own_in, preferred_element_type=jnp.float32),
            jnp.einsum("rf,df->rd", grad_pre, other_in, preferred_element_type=jnp.float32),
        ],
        axis=1,
    )
    unit_sum = swapped_sum(unit_parts, "tensor")
    grad_unit_in = parity_join(unit_sum[:, :half], unit_sum[:, half:], core, chips)
    scaled = grad_unit_in * ln_gain
    grad_rows = inv_std * (
        scaled
        - jnp.mean(scaled, axis=1, keepdims=True)
        - normal_rows * jnp.mean(scaled * normal_rows, axis=1, keepdims=True)
    )
    grad_pooled = (grad_mixed + grad_rows)[None]

    width = grad_pre.shape[1]
    terms_own = jnp.concatenate(
        [
            jnp.einsum("rd,rf->df", unit_own, grad_pre, preferred_element_type=jnp.float32),
            jnp.einsum("rd,rf->df", grad_own, hidden, preferred_element_type=jnp.float32),
        ],
        axis=1,
    )
    terms_other = jnp.concatenate(
        [
            jnp.einsum("rd,rf->df", unit_other, grad_pre, preferred_element_type=jnp.float32),
            jnp.einsum("rd,rf->df", grad_other, hidden, preferred_element_type=jnp.float32),
        ],
        axis=1,
    )
    terms_chip = terms_own.astype(jnp.bfloat16).astype(jnp.float32) + core_swap(
        terms_other.astype(jnp.bfloat16)
    ).astype(jnp.float32)
    terms_part = lax.psum_scatter(
        terms_chip.astype(jnp.bfloat16), "z", scatter_dimension=0, tiled=True
    )
    total = ring_dp_sum(terms_part)
    grad_in = total[:, :width]
    grad_out = total[:, width:].T
    return (grad_pooled, grad_in, grad_out)


def solution(mesh):
    fsdp = mesh.shape["fsdp"]
    chip_mesh = Mesh(
        mesh.devices.reshape(mesh.shape["dp"], fsdp // 2, 2, mesh.shape["tensor"]),
        ("dp", "z", "core", "tensor"),
    )
    placed = (
        P("dp", ("z", "core"), None),
        P(),
        P(("z", "core"), "tensor"),
        P("tensor", ("z", "core")),
        P("dp", ("z", "core", "tensor"), None),
    )
    return jax.shard_map(
        layer,
        mesh=chip_mesh,
        in_specs=placed,
        out_specs=(
            P("dp", ("z", "core"), None),
            P(("z", "core"), "tensor"),
            P("tensor", ("z", "core")),
        ),
        check_vma=False,
    )
```

```python
import jax
import jax.numpy as jnp
from jax import lax
from jax.sharding import Mesh
from jax.sharding import PartitionSpec as P


ln_eps = 1e-06
norm_eps = 1e-06
logit_scale = 10.0
logit_bias = -2.0


def passed_along(block, axis, distance):
    devices = range(lax.axis_size(axis))
    route = [((i - distance) % len(devices), i) for i in devices]
    return lax.ppermute(block, axis, route)


def core_swap(block):
    return lax.ppermute(block, "core", [(0, 1), (1, 0)])


def swapped_sum(partial, axis):
    mine = partial.astype(jnp.bfloat16)
    half = mine.shape[0] // 2
    other = jnp.concatenate(
        [
            lax.ppermute(mine[:half], axis, [(0, 1), (1, 0)]),
            lax.ppermute(mine[half:], axis, [(0, 1), (1, 0)]),
        ]
    )
    return mine.astype(jnp.float32) + other.astype(jnp.float32)


def doubling_sum(parts, axis):
    size = lax.axis_size(axis)
    mine = [p.astype(jnp.bfloat16) for p in parts]
    totals = None
    bit = 1
    while bit < size:
        route = [(i, i ^ bit) for i in range(size)]
        others = [lax.ppermute(m, axis, route) for m in mine]
        totals = [m.astype(jnp.float32) + o.astype(jnp.float32) for m, o in zip(mine, others)]
        mine = [t.astype(jnp.bfloat16) for t in totals]
        bit *= 2
    return totals


def parity_split(values, core, chips):
    lead = values.shape[:-1]
    blocks = values.reshape(lead + (chips, 2, values.shape[-1] // (2 * chips)))
    axis = blocks.ndim - 2
    own = lax.dynamic_index_in_dim(blocks, core, axis=axis, keepdims=False)
    other = lax.dynamic_index_in_dim(blocks, 1 - core, axis=axis, keepdims=False)
    half = lead + (values.shape[-1] // 2,)
    return own.reshape(half), other.reshape(half)


def parity_join(own, other, core, chips):
    lead = own.shape[:-1]
    shape = lead + (chips, 1, own.shape[-1] // chips)
    own = own.reshape(shape)
    other = other.reshape(shape)
    even = jnp.where(core == 0, own, other)
    odd = jnp.where(core == 0, other, own)
    return jnp.concatenate([even, odd], axis=-2).reshape(lead + (2 * own.shape[-1] * chips,))


def gelu_tanh(values):
    return jax.nn.gelu(values, approximate=True)


def unit_rows(values):
    return values / jnp.sqrt(jnp.sum(values * values, axis=-1, keepdims=True) + norm_eps)


def layer(pooled, ln_gain, w_in, w_out, texts):
    rows = pooled[0].astype(jnp.float32)
    images = rows.shape[0]
    chip = lax.axis_index("z")
    chips = lax.axis_size("z")
    core = lax.axis_index("core")
    block_index = chip * 2 + core

    text_b = unit_rows(texts[0].astype(jnp.float32)).astype(jnp.bfloat16)
    block_rows = text_b.shape[0]
    half_index = lax.axis_index("tensor")
    within = jnp.arange(block_rows, dtype=jnp.int32)

    def block_columns(source_chip, parity, half):
        return (source_chip * 2 + parity) * images + half * block_rows + within

    blocks = [text_b]
    sources = [chip]
    ahead = text_b
    for step in range(1, chips // 2 + 1):
        ahead = passed_along(ahead, "z", 1)
        blocks.append(ahead)
        sources.append((chip - step) % chips)
    behind = text_b
    for step in range(1, (chips - 1) // 2 + 1):
        behind = passed_along(behind, "z", -1)
        blocks.append(behind)
        sources.append((chip + step) % chips)
    own_texts = jnp.concatenate(blocks, axis=0)
    core_texts = jnp.concatenate([own_texts, core_swap(own_texts)], axis=0)
    all_texts = core_texts
    columns = jnp.concatenate(
        [block_columns(s, core, half_index) for s in sources]
        + [block_columns(s, 1 - core, half_index) for s in sources],
        axis=0,
    )

    stacked = jnp.stack([w_in, w_out.T])
    own_w = lax.all_gather(stacked, "z", axis=1, tiled=True)
    other_w = core_swap(own_w)
    own_in, own_out = own_w[0], own_w[1]
    other_in, other_out = other_w[0], other_w[1]

    row_mean = jnp.mean(rows, axis=1, keepdims=True)
    centred = rows - row_mean
    inv_std = lax.rsqrt(jnp.mean(centred * centred, axis=1, keepdims=True) + ln_eps)
    normal_rows = centred * inv_std
    unit_in = (normal_rows * ln_gain).astype(jnp.bfloat16)
    unit_own, unit_other = parity_split(unit_in, core, chips)
    pre_act = jnp.dot(unit_own, own_in, preferred_element_type=jnp.float32) + jnp.dot(
        unit_other, other_in, preferred_element_type=jnp.float32
    )
    hidden = gelu_tanh(pre_act).astype(jnp.bfloat16)
    mix_parts = jnp.concatenate(
        [
            jnp.einsum("rf,df->rd", hidden, own_out, preferred_element_type=jnp.float32),
            jnp.einsum("rf,df->rd", hidden, other_out, preferred_element_type=jnp.float32),
        ],
        axis=1,
    )
    mix_sum = swapped_sum(mix_parts, "tensor")
    half = mix_sum.shape[1] // 2
    mixed = rows + parity_join(mix_sum[:, :half], mix_sum[:, half:], core, chips)
    row_norm = jnp.sqrt(jnp.sum(mixed * mixed, axis=1, keepdims=True) + norm_eps)
    image_unit = mixed / row_norm
    image_b = image_unit.astype(jnp.bfloat16)
    image_places = block_index * images + jnp.arange(images, dtype=jnp.int32)

    logits = (
        logit_scale
        * jnp.einsum("rd,cd->rc", image_b, all_texts, preferred_element_type=jnp.float32)
        + logit_bias
    )
    match = (image_places[:, None] == columns[None, :]).astype(jnp.float32)
    weights = (jax.nn.sigmoid(logits) - match).astype(jnp.bfloat16)
    running = jnp.dot(weights, all_texts, preferred_element_type=jnp.float32)
    grad_unit = swapped_sum(logit_scale * running, "tensor")
    grad_mixed = (
        grad_unit - image_unit * jnp.sum(image_unit * grad_unit, axis=1, keepdims=True)
    ) / row_norm
    grad_b = grad_mixed.astype(jnp.bfloat16)
    grad_own, grad_other = parity_split(grad_b, core, chips)
    grad_hidden = jnp.einsum(
        "rd,df->rf", grad_own, own_out, preferred_element_type=jnp.float32
    ) + jnp.einsum("rd,df->rf", grad_other, other_out, preferred_element_type=jnp.float32)
    _, gelu_back = jax.vjp(gelu_tanh, pre_act)
    grad_pre = gelu_back(grad_hidden)[0].astype(jnp.bfloat16)
    unit_parts = jnp.concatenate(
        [
            jnp.einsum("rf,df->rd", grad_pre, own_in, preferred_element_type=jnp.float32),
            jnp.einsum("rf,df->rd", grad_pre, other_in, preferred_element_type=jnp.float32),
        ],
        axis=1,
    )
    unit_sum = swapped_sum(unit_parts, "tensor")
    grad_unit_in = parity_join(unit_sum[:, :half], unit_sum[:, half:], core, chips)
    scaled = grad_unit_in * ln_gain
    grad_rows = inv_std * (
        scaled
        - jnp.mean(scaled, axis=1, keepdims=True)
        - normal_rows * jnp.mean(scaled * normal_rows, axis=1, keepdims=True)
    )
    grad_pooled = (grad_mixed + grad_rows)[None]

    width = grad_pre.shape[1]
    terms_own = jnp.concatenate(
        [
            jnp.einsum("rd,rf->df", unit_own, grad_pre, preferred_element_type=jnp.float32),
            jnp.einsum("rd,rf->df", grad_own, hidden, preferred_element_type=jnp.float32),
        ],
        axis=1,
    )
    terms_other = jnp.concatenate(
        [
            jnp.einsum("rd,rf->df", unit_other, grad_pre, preferred_element_type=jnp.float32),
            jnp.einsum("rd,rf->df", grad_other, hidden, preferred_element_type=jnp.float32),
        ],
        axis=1,
    )
    terms_chip = terms_own.astype(jnp.bfloat16).astype(jnp.float32) + core_swap(
        terms_other.astype(jnp.bfloat16)
    ).astype(jnp.float32)
    terms_part = lax.psum_scatter(
        terms_chip.astype(jnp.bfloat16), "z", scatter_dimension=0, tiled=True
    )
    (total,) = doubling_sum([terms_part], "dp")
    grad_in = total[:, :width]
    grad_out = total[:, width:].T
    return (grad_pooled, grad_in, grad_out)


def solution(mesh):
    fsdp = mesh.shape["fsdp"]
    chip_mesh = Mesh(
        mesh.devices.reshape(mesh.shape["dp"], fsdp // 2, 2, mesh.shape["tensor"]),
        ("dp", "z", "core", "tensor"),
    )
    placed = (
        P("dp", ("z", "core"), None),
        P(),
        P(("z", "core"), "tensor"),
        P("tensor", ("z", "core")),
        P("dp", ("z", "core", "tensor"), None),
    )
    return jax.shard_map(
        layer,
        mesh=chip_mesh,
        in_specs=placed,
        out_specs=(
            P("dp", ("z", "core"), None),
            P(("z", "core"), "tensor"),
            P("tensor", ("z", "core")),
        ),
        check_vma=False,
    )
```
